32 devices in a mesh: grp: 4 (over y, core), node: 8 (over z, x).
Axes of the slice: x: 2, y: 2, z: 4, core: 2. Of those that a mesh axis runs over, the one named last changes fastest.
Arguments:
- excitation: float32 [128, 32768], P(None, ('grp', 'node')), may hold values from -6 to 6
- points: float32 [3, 32768], P(None, ('grp', 'node')), may hold values from -5 to 5
- near_mask: int32 [32, 2], P(('grp', 'node')), may hold values from 0 to 1, as said below
- bit_order: int32 [3], replicated, may hold values from 0 to 2, as said below
- compress: float32 [32768, 256], P(('grp', 'node')), may hold values from -0.1875 to 0.1875
- level_self: float32 [3, 8192, 256], P(None, ('grp', 'node')), may hold values from -0.25 to 0.25
- level_partner: float32 [3, 8192, 256], P(None, ('grp', 'node')), may hold values from -0.25 to 0.25
- expand: float32 [8192, 4096], P(('grp', 'node')), may hold values from -0.375 to 0.375
Outputs:
- field: float32 [128, 32768], P(None, ('grp', 'node'))
The draws below stay inside these ranges and needn't reach their ends.
Inputs may be any that keep to these rules, and one draw needn't show every extreme that they name: near_mask[b, 0] is 0 when b is the first cluster of its group and near_mask[b, 1] is 0 when b is the last; otherwise each entry is 0 or 1. `bit_order`: the entries are distinct bits of a node index; each of 0 to 2 appears once.
All inputs are finite; a program needn't handle non-finite values.
Results may differ from the reference program's by a relative error of at most 0.0001.
Values sent between devices are 32-bit elements; how exact they have to be, the bound alone decides.
No kernel may reach another device: no remote copies, remote signals or barrier semaphores. Data moves between devices by JAX's collectives and lax.ppermute only.
A program may use at most 64 MiB of HBM per device.

```python
import math
import jax
import jax.numpy as jnp
from jax import lax

BLOCK = 1024
RANK = 256
COLS = 128
LEVELS = 3
BLOCKS = 32
ROWS = 32768
GROUP_ROWS = 4096
N_GRP = 4
N_NODE = 8


def draw_near_mask(key, part):
    flags = jax.random.randint(jax.random.fold_in(key, 11), (BLOCKS, 2), 0, 2).astype(jnp.int32)
    position = jnp.arange(BLOCKS, dtype=jnp.int32) % N_NODE
    first = (position != 0).astype(jnp.int32)
    last = (position != N_NODE - 1).astype(jnp.int32)
    return jnp.stack([flags[:, 0] * first, flags[:, 1] * last], axis=1)


def draw_bit_order(key, part):
    return jax.random.permutation(jax.random.fold_in(key, 23), LEVELS).astype(jnp.int32)


def block_levels(key, extent, cuts, least, largest):
    level = 1.0
    for axis_at, parts in cuts:
        steps = jax.random.uniform(jax.random.fold_in(jax.random.fold_in(key, 6), axis_at), (parts,), jnp.float32, least / len(cuts), largest / len(cuts))
        level = level * jnp.repeat(jnp.exp(steps), extent[axis_at] // parts).reshape((-1,) + (1,) * (len(extent) - 1 - axis_at))
    return level


def gaussian(key, shape, width, most, split=(), held_as=jnp.bfloat16):
    factor_of = block_levels(key, shape, split, -0.22, 0.18) if split else 1.0
    result = jax.random.normal(key, shape, jnp.float32) * width * factor_of
    return jnp.minimum(jnp.maximum(result, -most), most).astype(held_as)


def setup_inputs(seed: int = 0) -> dict:
    key_of = jax.random.split(jax.random.key(seed), 9)
    excitation = gaussian(key_of[0], (COLS, ROWS), 1.0, 6.0, ((1, 32),), jnp.float32)
    points = gaussian(key_of[1], (3, ROWS), 1.0, 5.0, ((1, 32),), jnp.float32)
    near_mask = draw_near_mask(jax.random.fold_in(key_of[8], 71), 0)
    bit_order = draw_bit_order(jax.random.fold_in(key_of[8], 71), 0)
    compress = gaussian(key_of[4], (ROWS, RANK), BLOCK ** -0.5, 0.1875, ((0, 32),), jnp.float32)
    level_self = gaussian(key_of[5], (LEVELS, BLOCKS * RANK, RANK), (2 * RANK) ** -0.5, 0.25, ((1, 32),), jnp.float32)
    level_partner = gaussian(key_of[6], (LEVELS, BLOCKS * RANK, RANK), (2 * RANK) ** -0.5, 0.25, ((1, 32),), jnp.float32)
    expand = gaussian(key_of[7], (BLOCKS * RANK, GROUP_ROWS), RANK ** -0.5, 0.375, ((0, 32),), jnp.float32)
    return dict(excitation=excitation, points=points, near_mask=near_mask, bit_order=bit_order, compress=compress, level_self=level_self, level_partner=level_partner, expand=expand)


HIGH = lax.Precision.HIGHEST
SOFTEN = 0.01

def kernel_block(sources, targets):
    dist_sq = (sources[0][:, None] - targets[0][None, :]) ** 2
    dist_sq = dist_sq + (sources[1][:, None] - targets[1][None, :]) ** 2
    dist_sq = dist_sq + (sources[2][:, None] - targets[2][None, :]) ** 2
    return lax.rsqrt(dist_sq + SOFTEN) * (1.0 / math.sqrt(sources.shape[1]))

def reference(excitation, points, near_mask, bit_order, compress, level_self, level_partner, expand):
    blocked = excitation.reshape(COLS, BLOCKS, BLOCK).transpose(1, 0, 2)
    coords = points.reshape(3, BLOCKS, BLOCK).transpose(1, 0, 2)
    comp = compress.reshape(BLOCKS, BLOCK, RANK)
    state = jnp.einsum('bcr,brk->bck', blocked, comp, precision=HIGH)
    selfs = level_self.reshape(LEVELS, BLOCKS, RANK, RANK)
    others = level_partner.reshape(LEVELS, BLOCKS, RANK, RANK)
    labels = jnp.arange(BLOCKS, dtype=jnp.int32)
    for level in range(LEVELS):
        partner = jnp.bitwise_xor(labels, jnp.left_shift(jnp.int32(1), bit_order[level]).astype(jnp.int32))
        moved = jnp.take(state, partner, axis=0)
        state = jnp.einsum('bck,bkr->bcr', state, selfs[level], precision=HIGH) + jnp.einsum('bck,bkr->bcr', moved, others[level], precision=HIGH)
    grouped = state.reshape(N_GRP, N_NODE, COLS, RANK)
    maps = expand.reshape(N_GRP, N_NODE, RANK, N_GRP, BLOCK)
    far = jnp.einsum('gncr,gnrhk->hnck', grouped, maps, precision=HIGH).reshape(BLOCKS, COLS, BLOCK)
    flags = near_mask.astype(jnp.float32)
    before_x = jnp.roll(blocked, 1, axis=0)
    after_x = jnp.roll(blocked, -1, axis=0)
    before_p = jnp.roll(coords, 1, axis=0)
    after_p = jnp.roll(coords, -1, axis=0)

    def near_one(items):
        own_x, own_p, left_x, left_p, right_x, right_p, flag = items
        total = jnp.dot(own_x, kernel_block(own_p, own_p), precision=HIGH)
        total = total + flag[0] * jnp.dot(left_x, kernel_block(left_p, own_p), precision=HIGH)
        total = total + flag[1] * jnp.dot(right_x, kernel_block(right_p, own_p), precision=HIGH)
        return total
    near = lax.map(near_one, (blocked, coords, before_x, before_p, after_x, after_p, flags))
    return (far + near).transpose(1, 0, 2).reshape(COLS, ROWS)
```

```python
import functools
import itertools
import math

import jax
import jax.numpy as jnp
from jax import lax
from jax.sharding import PartitionSpec as P

HIGH = lax.Precision.HIGH
SOFTEN = 0.01
MOST_ORDERS = 6


def swapped(block, axis, bit):
    count = lax.axis_size(axis)
    return lax.ppermute(block, axis, [(i, i ^ 1 << bit) for i in range(count) if i ^ 1 << bit < count])


def dot(left, right):
    return jnp.dot(left, right, precision=HIGH)


def kernel_block(sources, targets):
    dist_sq = (sources[0][:, None] - targets[0][None, :]) ** 2
    dist_sq = dist_sq + (sources[1][:, None] - targets[1][None, :]) ** 2
    dist_sq = dist_sq + (sources[2][:, None] - targets[2][None, :]) ** 2
    return lax.rsqrt(dist_sq + SOFTEN) * (1.0 / math.sqrt(sources.shape[1]))


def level_step(state, own, other, bit):
    moved = swapped(state, "node", bit)
    return dot(state, own) + dot(moved, other)


def butterfly(state, level_self, level_partner, bit_order):
    levels = level_self.shape[0]
    bits = lax.axis_size("node").bit_length() - 1
    orders = list(itertools.permutations(range(bits), levels))
    if len(orders) > MOST_ORDERS:
        for level in range(levels):
            steps = [functools.partial(level_step, bit=bit) for bit in range(bits)]
            state = lax.switch(bit_order[level], steps, state, level_self[level], level_partner[level])
        return state

    def whole(order):
        def run(state):
            for level, bit in enumerate(order):
                state = level_step(state, level_self[level], level_partner[level], bit)
            return state

        return run

    which = sum(
        jnp.all(bit_order == jnp.array(order, jnp.int32)).astype(jnp.int32) * at
        for at, order in enumerate(orders)
    )
    return lax.switch(which, [whole(order) for order in orders], state)


def shards(excitation, points, near_mask, bit_order, compress, level_self, level_partner, expand):
    cols, width = excitation.shape
    rank = compress.shape[1]
    nodes, groups = lax.axis_size("node"), lax.axis_size("grp")
    node, group = lax.axis_index("node"), lax.axis_index("grp")
    flags = near_mask[0].astype(jnp.float32)

    packed = jnp.concatenate([excitation, points], axis=0)
    first = swapped(packed, "node", 0)
    route = [(i, i + 2) for i in range(0, nodes - 2, 2)] + [(i, i - 2) for i in range(3, nodes, 2)]
    second = lax.ppermute(first, "node", route)
    odd = node % 2
    first_flag = jnp.where(odd == 1, flags[0], flags[1])
    second_flag = jnp.where(odd == 1, flags[1], flags[0])

    other_expand = swapped(expand, "grp", 0)

    state = dot(excitation, compress)
    state = butterfly(state, level_self, level_partner, bit_order)
    other_state = swapped(state, "grp", 0)

    def share(target):
        own_cols = lax.dynamic_slice_in_dim(expand, target * width, width, axis=1)
        other_cols = lax.dynamic_slice_in_dim(other_expand, target * width, width, axis=1)
        return dot(state, own_cols) + dot(other_state, other_cols)

    apart = groups // 2
    total = None
    ring = groups // 2
    bits = ring.bit_length() - 1
    held = [share(group ^ (k << 1)) for k in reversed(range(ring))]
    held = held[::-1]
    for bit in reversed(range(bits)):
        half = 1 << bit
        away = held[half:]
        held = held[:half]
        got = [swapped(piece, "grp", bit + 1) for piece in away]
        held = [a + b for a, b in zip(held, got)]
    far = held[0]

    def near_term(block, flag):
        return dot(block[:cols] * flag, kernel_block(block[cols:], points))

    near = dot(excitation, kernel_block(points, points))
    near = near + near_term(first, first_flag) + near_term(second, second_flag)
    return far + near


def solution(mesh):
    return jax.shard_map(
        shards,
        mesh=mesh,
        in_specs=(
            P(None, ("grp", "node")),
            P(None, ("grp", "node")),
            P(("grp", "node"), None),
            P(),
            P(("grp", "node"), None),
            P(None, ("grp", "node"), None),
            P(None, ("grp", "node"), None),
            P(("grp", "node"), None),
        ),
        out_specs=P(None, ("grp", "node")),
        check_vma=False,
    )
```
